256 devices in a mesh: dp: 8 (over x_hi, y), tp: 32 (over x_lo, z, core).
Axes of the slice: x: 4 (x_hi: 2, x_lo: 2; x = x_hi * 2 + x_lo), y: 4, z: 8, core: 2. Of those that a mesh axis runs over, the one named last changes fastest.
Arguments:
- hidden: bfloat16 [6144, 2880], P(('dp', 'tp')), parts along dimension 0, may hold values from -6 to 6
- attn_gain: float32 [2880], replicated, may hold values from 0.1 to 1.9
- w_query: bfloat16 [2880, 4096], P(None, 'tp'), may hold values from -0.109375 to 0.109375
- w_keyval: bfloat16 [2880, 1024], P(None, 'tp'), may hold values from -0.109375 to 0.109375
- w_out: bfloat16 [4096, 2880], P('tp'), may hold values from -0.09375 to 0.09375
- cache_keys: bfloat16 [256, 2048, 512], P(('dp', 'tp')), parts along dimension 0, may hold values from -70 to 70
- cache_values: bfloat16 [256, 2048, 512], P(('dp', 'tp')), parts along dimension 0, may hold values from -6 to 6
- cache_lens: int32 [256], P(('dp', 'tp')), parts along dimension 0, may hold values from 256 to 2048, as said below
- parents: int32 [256, 24], P(('dp', 'tp')), parts along dimension 0, may hold values from 0 to 23, as said below
- accepted: int32 [256], P(('dp', 'tp')), parts along dimension 0, may hold values from 0 to 23, as said below
- moe_gain: float32 [2880], replicated, may hold values from 0.1 to 1.9
- w_router: bfloat16 [2880, 32], replicated, may hold values from -0.109375 to 0.109375
- routes: int32 [6144, 4], P('dp'), parts along dimension 0, may hold values from 0 to 31, all different within a row; in each aligned block of 768 rows (0 to 767, 768 to 1535, ...) at most 192 rows name the same one
- w_gate: bfloat16 [11520, 2880], P('tp'), may hold values from -0.109375 to 0.109375
- w_up: bfloat16 [11520, 2880], P('tp'), may hold values from -0.109375 to 0.109375
- w_down: bfloat16 [11520, 2880], P('tp'), may hold values from -0.109375 to 0.109375
Outputs:
- layer_out: bfloat16 [6144, 2880], P(('dp', 'tp')), parts along dimension 0
- accepted_kv: bfloat16 [256, 8, 1024], P(('dp', 'tp')), parts along dimension 0
The draws below stay inside these ranges and needn't reach their ends.
There are 8 independent parts, one for each index of `dp`. The reference program is written for one: setup_inputs(seed, part) draws one part's arguments, and reference() takes and returns one part's arrays. A program takes and returns all parts, laid end to end along the dimension named above; an argument that names none is the same for every part. Nothing has to cross between parts.
Inputs may be any that keep to these rules, and one draw needn't show every extreme that they name: `cache_lens`: 2048 for at least one request of every part. `parents`: node 0 names itself; every other node names a node of smaller index; no path from node 0 holds more than 8 nodes, and every tree has one of exactly 8. The path from node 0 to the accepted node holds at most 8 nodes, exactly 8 for at least one request of every part. `routes`: each token names 4 different experts; at most 192 tokens of a part name any one expert, a bound that some block reaches.
All inputs are finite; a program needn't handle non-finite values.
Results may differ from the reference program's by a relative error of at most 0.012.
The reference program's roundings to bfloat16 on the way count: a program that leaves them out, or rounds other values in their place, can miss the bound.
Values may be sent and summed in bfloat16 or wider, within the bound.
A program may use at most 128 MiB of HBM per device.

```python
import math
import jax
import jax.numpy as jnp
import numpy as np
from jax import lax

D = 2880
HEADS = 64
KV_HEADS = 8
HEAD_DIM = 64
EXPERTS = 32
EXPERT_HID = 2880
TOP = 4
EXP_WIN = 4
DRAFT = 24
DEPTH = 8
CACHE = 2048
REQS = 32
TOKENS = 768
CAP = 192


def draw_cache_keys(key, part):
    shape = (REQS, CACHE, KV_HEADS * HEAD_DIM)
    base = jax.random.normal(key, shape, jnp.float32)
    return jnp.clip(base, -6.0, 6.0).astype(jnp.bfloat16)


def draw_cache_lens(key, part):
    lengths = jax.random.randint(key, (REQS,), CACHE // 8, CACHE + 1)
    longest = jax.random.randint(jax.random.fold_in(key, 3), (), 0, REQS)
    return jnp.where(jnp.arange(REQS) == longest, CACHE, lengths).astype(jnp.int32)


def draw_parents(key, part):
    parent_cols = [jnp.zeros((REQS,), jnp.int32)]
    depth_cols = [jnp.zeros((REQS,), jnp.int32)]
    for node in range(1, DRAFT):
        so_far = jnp.stack(depth_cols, axis=1)
        if node < DEPTH:
            picked = jnp.full((REQS,), node - 1, jnp.int32)
        else:
            scores = jax.random.randint(jax.random.fold_in(key, node), (REQS, node), 0, 4096) * node + jnp.arange(node)
            eligible = so_far < DEPTH - 1
            picked = jnp.argmax(jnp.where(eligible, scores, -1), axis=1).astype(jnp.int32)
        depth_new = jnp.take_along_axis(so_far, picked[:, None], axis=1)[:, 0] + 1
        parent_cols.append(picked)
        depth_cols.append(depth_new.astype(jnp.int32))
    return jnp.stack(parent_cols, axis=1).astype(jnp.int32)


def draw_accepted(key, part):
    leaves = jax.random.randint(key, (REQS,), 0, DRAFT)
    deepest = jax.random.randint(jax.random.fold_in(key, 5), (), 0, REQS)
    return jnp.where(jnp.arange(REQS) == deepest, DEPTH - 1, leaves).astype(jnp.int32)


def levels(key, extent, split, low, largest):
    level = 1.0
    for dim, parts in split:
        steps = jax.random.uniform(jax.random.fold_in(jax.random.fold_in(key, 6), dim), (parts,), jnp.float32, low / len(split), largest / len(split))
        level = level * jnp.repeat(jnp.exp(steps), extent[dim] // parts).reshape((-1,) + (1,) * (len(extent) - 1 - dim))
    return level


def assign_block(stream_key, own, number, rows, number_of, top, bound, slope):
    ranking = jax.random.permutation(stream_key, number_of)
    crowded, common = load_shares(number_of, rows * top, bound, slope, True), load_shares(number_of, rows * top, bound, slope, False)
    places = jnp.arange(number_of)

    def named(sizes, offset_by):
        used = int((sizes > 0).sum())
        fixed = max(1, used // 4)
        passed = fixed + (places - fixed + offset_by * (used - fixed)) % max(1, number_of - fixed)
        return jnp.zeros((number_of,), jnp.int32).at[ranking[jnp.where(places < fixed, places, passed)]].set(jnp.asarray(sizes, jnp.int32))

    sizes = jnp.where(number % 4 == 0, named(crowded, number // 4), named(common, number - number // 4 - 1))
    mixed = jax.random.permutation(jax.random.fold_in(own, 3), number_of)
    donor, receiver = mixed[0:number_of // 2 * 2:2], mixed[1:number_of // 2 * 2:2]
    room = jnp.minimum(sizes[donor] - 1, bound - sizes[receiver]) // 2
    room = jnp.where((donor == ranking[0]) | (receiver == ranking[0]) | (sizes[receiver] == 0), 0, jnp.maximum(room, 0))
    passed = jax.random.randint(jax.random.fold_in(own, 4), (number_of // 2,), 0, 1 << 20) % (room + 1)
    sizes = sizes.at[donor].add(-passed).at[receiver].add(passed)
    items = jnp.searchsorted(jnp.cumsum(sizes), jnp.arange(rows * top), side="right").astype(jnp.int32)
    table = items.reshape(top, rows).T
    table = table[jax.random.permutation(jax.random.fold_in(own, 1), rows)]
    offset_by = jax.random.randint(jax.random.fold_in(own, 2), (rows, 1), 0, top)
    return jnp.take_along_axis(table, (jnp.arange(top)[None, :] + offset_by) % top, axis=1)


def load_shares(count, total, most, slope, full):
    portions = [(1 << 20) // math.isqrt(grade ** slope) + 1 for grade in range(1, count + 1)]
    largest = most if full else min(most, max(-(-total // count), total * portions[0] // sum(portions)))
    least = 1 if total - largest >= count - 1 else 0
    holding, spare = [largest] + [least] * (count - 1), total - largest - least * (count - 1)
    while spare > 0:
        candidates = [i for i in range(1, count) if holding[i] < largest] or [i for i in range(1, count) if holding[i] < most]
        whole, budget = sum([portions[i] for i in candidates]), spare
        for i in candidates:
            more = min(most - holding[i], max(1, budget * portions[i] // whole), spare)
            holding[i] = holding[i] + more
            spare = spare - more
    return np.array(holding)


def gaussian(stream_key, extent, spread, limit, shards=(), kind=jnp.bfloat16):
    factor_of = levels(stream_key, extent, shards, -0.22, 0.18) if shards else 1.0
    entries = jax.random.normal(stream_key, extent, jnp.float32) * spread * factor_of
    return jnp.minimum(jnp.maximum(entries, -limit), limit).astype(kind)


def setup_inputs(seed: int = 0, part: int = 0) -> dict:
    keys = jax.random.split(jax.random.key(seed), 17)
    part_keys = jax.random.split(jax.random.fold_in(keys[16], part), 17)
    hidden = gaussian(part_keys[0], (TOKENS, D), 1.0, 6.0, ((0, 32),))
    attn_gain = jnp.clip(1.0 + 0.18 * jax.random.normal(keys[1], (D,), jnp.float32), 0.1, 1.9)
    w_query = gaussian(keys[2], (D, HEADS * HEAD_DIM), D ** -0.5, 0.109375, ((1, 32),))
    w_keyval = gaussian(keys[3], (D, 2 * KV_HEADS * HEAD_DIM), D ** -0.5, 0.109375, ((1, 32),))
    w_out = gaussian(keys[4], (HEADS * HEAD_DIM, D), (HEADS * HEAD_DIM) ** -0.5, 0.09375, ((0, 32),))
    cache_keys = draw_cache_keys(jax.random.fold_in(jax.random.fold_in(keys[16], part), 71), part)
    cache_values = gaussian(part_keys[6], (REQS, CACHE, KV_HEADS * HEAD_DIM), 1.0, 6.0, ((0, 32),))
    cache_lens = draw_cache_lens(jax.random.fold_in(jax.random.fold_in(keys[16], part), 71), part)
    parents = draw_parents(jax.random.fold_in(jax.random.fold_in(keys[16], part), 71), part)
    accepted = draw_accepted(jax.random.fold_in(jax.random.fold_in(keys[16], part), 71), part)
    moe_gain = jnp.clip(1.0 + 0.18 * jax.random.normal(keys[10], (D,), jnp.float32), 0.1, 1.9)
    w_router = gaussian(keys[11], (D, EXPERTS), D ** -0.5, 0.109375)
    routes_keys = jax.random.split(jax.random.fold_in(part_keys[12], 1), TOKENS // TOKENS)
    routes_turns = jax.random.permutation(jax.random.fold_in(part_keys[12], 3), TOKENS // TOKENS)
    routes = jax.vmap(lambda own, number: assign_block(jax.random.fold_in(part_keys[12], 2), own, number, TOKENS, EXPERTS, TOP, CAP, 2))(routes_keys, routes_turns).reshape((TOKENS, TOP))
    w_gate = gaussian(keys[13], (EXP_WIN * EXPERT_HID, D), D ** -0.5, 0.109375, ((0, 32),))
    w_up = gaussian(keys[14], (EXP_WIN * EXPERT_HID, D), D ** -0.5, 0.109375, ((0, 32),))
    w_down = gaussian(keys[15], (EXP_WIN * EXPERT_HID, D), EXPERT_HID ** -0.5, 0.109375, ((0, 32),))
    return {"hidden": hidden, "attn_gain": attn_gain, "w_query": w_query, "w_keyval": w_keyval, "w_out": w_out, "cache_keys": cache_keys, "cache_values": cache_values, "cache_lens": cache_lens, "parents": parents, "accepted": accepted, "moe_gain": moe_gain, "w_router": w_router, "routes": routes, "w_gate": w_gate, "w_up": w_up, "w_down": w_down}


THETA = 150000.0
SWIGLU_ALPHA = 1.702
EPSILON = 1e-05

def rms_norm(values, gain):
    floats = values.astype(jnp.float32)
    mean_sq = lax.optimization_barrier(jnp.mean(floats * floats, axis=-1, keepdims=True))
    return (floats * lax.rsqrt(mean_sq + EPSILON) * gain).astype(jnp.bfloat16)

def tree_paths(parent_row, depth_limit):
    count = parent_row.shape[0]
    identity = jnp.eye(count, dtype=jnp.bool_)
    ancestry = identity
    for level in range(depth_limit):
        ancestry = identity | jnp.take(ancestry, parent_row, axis=0)
    depths = lax.optimization_barrier(jnp.sum(ancestry.astype(jnp.int32), axis=1)) - 1
    return (ancestry, depths)

def rotate(values, positions):
    half = values.shape[-1] // 2
    steps_f = jnp.arange(half).astype(jnp.float32)
    inverse = jnp.exp(steps_f * (-2.0 * math.log(THETA) / values.shape[-1]))
    angles = positions[:, None] * inverse[None, :]
    cosine = jnp.cos(angles)[:, None, :]
    sine = jnp.sin(angles)[:, None, :]
    first = values[..., :half].astype(jnp.float32)
    second = values[..., half:].astype(jnp.float32)
    turned = jnp.concatenate([first * cosine - second * sine, second * cosine + first * sine], axis=-1)
    return turned.astype(jnp.bfloat16)

def rounded_float(values):
    return lax.optimization_barrier(values.astype(jnp.bfloat16)).astype(jnp.float32)

def attend_request(query, keyval, keys_cache, values_cache, length, parent_row, leaf, depth_limit):
    draft, heads, head_dim = query.shape
    kv_width = keyval.shape[1] // 2
    kv_heads = kv_width // head_dim
    ancestry, depths = tree_paths(parent_row, depth_limit)
    positions = (length + depths).astype(jnp.float32)
    query_rot = rotate(query, positions)
    new_keys = rotate(keyval[:, :kv_width].reshape(draft, kv_heads, head_dim), positions)
    new_values = keyval[:, kv_width:].reshape(draft, kv_heads, head_dim)
    grouped = query_rot.reshape(draft, kv_heads, heads // kv_heads, head_dim).astype(jnp.float32)
    scale = 1.0 / math.sqrt(head_dim)
    draft_scores = jnp.einsum('jgqd,kgd->gqjk', grouped, new_keys.astype(jnp.float32)) * scale
    draft_scores = jnp.where(ancestry[None, None], draft_scores, -jnp.inf)
    slots = keys_cache.shape[0]
    cache_k = keys_cache.reshape(slots, kv_heads, head_dim).astype(jnp.float32)
    cache_v = values_cache.reshape(slots, kv_heads, head_dim).astype(jnp.float32)
    cache_scores = jnp.einsum('jgqd,pgd->gqjp', grouped, cache_k) * scale
    live = jnp.arange(slots) < length
    cache_scores = jnp.where(live[None, None, None], cache_scores, -jnp.inf)
    top = jnp.maximum(lax.optimization_barrier(jnp.max(draft_scores, axis=-1)), lax.optimization_barrier(jnp.max(cache_scores, axis=-1)))
    draft_exp = jnp.exp(draft_scores - top[..., None])
    cache_exp = jnp.exp(cache_scores - top[..., None])
    total = lax.optimization_barrier(jnp.sum(draft_exp, axis=-1)) + lax.optimization_barrier(jnp.sum(cache_exp, axis=-1))
    weighted = jnp.einsum('gqjk,kgd->jgqd', rounded_float(draft_exp), new_values.astype(jnp.float32))
    weighted = weighted + jnp.einsum('gqjp,pgd->jgqd', rounded_float(cache_exp), cache_v)
    output = (weighted / jnp.transpose(total, (2, 0, 1))[..., None]).astype(jnp.bfloat16).reshape(draft, heads * head_dim)
    selector = ancestry[leaf][None, :] & (depths[None, :] == jnp.arange(depth_limit)[:, None])
    new_rows = jnp.concatenate([new_keys.reshape(draft, kv_width), new_values.reshape(draft, kv_width)], axis=1)
    accepted_rows = jnp.dot(selector.astype(jnp.bfloat16), new_rows, preferred_element_type=jnp.float32).astype(jnp.bfloat16)
    return (output, accepted_rows)

def gate_weights(inputs, router, routes):
    logits = jnp.dot(inputs, router, preferred_element_type=jnp.float32)
    onehot = routes[:, :, None] == jnp.arange(router.shape[1])[None, None, :]
    picked = lax.optimization_barrier(jnp.sum(jnp.where(onehot, logits[:, None, :], 0.0), axis=2))
    return jax.nn.softmax(picked, axis=1).astype(jnp.bfloat16)

def expert_term(inputs, weights, routes, expert, gate_rows, up_rows, down_rows, capacity):
    count = inputs.shape[0]
    match = routes == expert
    hits = jnp.any(match, axis=1)
    gate_of = lax.optimization_barrier(jnp.sum(jnp.where(match, weights.astype(jnp.float32), 0.0), axis=1))
    slot_ids = jnp.cumsum(hits.astype(jnp.int32)) - 1
    target = jnp.where(hits, slot_ids, capacity).astype(jnp.int32)
    index = jnp.full((capacity,), count, jnp.int32).at[target].set(jnp.arange(count).astype(jnp.int32), mode='drop')
    valid = index < count
    safe = jnp.minimum(index, count - 1)
    picked = inputs[safe]
    gate_val = lax.dot_general(picked, gate_rows, (((1,), (1,)), ((), ())), preferred_element_type=jnp.float32)
    up_val = lax.dot_general(picked, up_rows, (((1,), (1,)), ((), ())), preferred_element_type=jnp.float32)
    active = (gate_val * jax.nn.sigmoid(SWIGLU_ALPHA * gate_val) * (up_val + 1.0)).astype(jnp.bfloat16)
    result = jnp.dot(active, down_rows, preferred_element_type=jnp.float32)
    scale_rows = jnp.where(valid, gate_of[safe], 0.0)
    empty = jnp.zeros((count, inputs.shape[1]), jnp.float32)
    return empty.at[index].add(result * scale_rows[:, None], mode='drop')

def reference(hidden, attn_gain, w_query, w_keyval, w_out, cache_keys, cache_values, cache_lens, parents, accepted, moe_gain, w_router, routes, w_gate, w_up, w_down):
    normed = rms_norm(hidden, attn_gain)
    query = jnp.dot(normed, w_query, preferred_element_type=jnp.float32).astype(jnp.bfloat16)
    keyval = jnp.dot(normed, w_keyval, preferred_element_type=jnp.float32).astype(jnp.bfloat16)
    query = query.reshape(REQS, DRAFT, HEADS, HEAD_DIM)
    keyval = keyval.reshape(REQS, DRAFT, 2 * KV_HEADS * HEAD_DIM)

    def per_request(items):
        return attend_request(*items, DEPTH)
    attended, accepted_kv = lax.map(per_request, (query, keyval, cache_keys, cache_values, cache_lens, parents, accepted))
    attended = attended.reshape(TOKENS, HEADS * HEAD_DIM)
    middle = (hidden.astype(jnp.float32) + jnp.dot(attended, w_out, preferred_element_type=jnp.float32)).astype(jnp.bfloat16)
    moe_in = rms_norm(middle, moe_gain)
    weights = gate_weights(moe_in, w_router, routes)
    summed = jnp.zeros((TOKENS, D), jnp.float32)
    for expert in range(EXP_WIN):
        first = expert * EXPERT_HID
        last = first + EXPERT_HID
        summed = summed + expert_term(moe_in, weights, routes, expert, w_gate[first:last], w_up[first:last], w_down[first:last], CAP)
    layer_out = (middle.astype(jnp.float32) + summed).astype(jnp.bfloat16)
    return (layer_out, accepted_kv)
```

```python
import functools
import math

import jax
import jax.numpy as jnp
from jax import lax
from jax.experimental import pallas as pl
from jax.experimental.pallas import tpu as pltpu
from jax.sharding import PartitionSpec as P

HEADS = 64
HEAD_DIM = 64
EXPERT_HID = 2880
DEPTH = 8


THETA = 150000.0
SWIGLU_ALPHA = 1.702
EPSILON = 1e-05

MESH = pl.DeviceIdType.MESH
RING = 8
OFFSETS = (0, 1, -1, 2, -2, 3, -3, 4)
MIRROR = (0, 2, 1, 4, 3, 6, 5, 7)
LEVELS = ((0,), (1, 2), (3, 4), (5, 6), (7,))


def split_of(width):
    return (width // 2) // 128 * 128


class Place:
    def __init__(self):
        self.t = lax.axis_index("tp")
        self.c = lax.rem(self.t, 2)
        self.z = lax.rem(self.t // 2, RING)
        self.x = self.t // (2 * RING)
        self.forward = 1 - 2 * self.c

    def at(self, row, offset, core=None):
        z = lax.rem(self.z + self.forward * offset + 2 * RING, RING)
        x = self.x if row == 0 else 1 - self.x
        return (x * RING + z) * 2 + (self.c if core is None else core)

    def neighbours(self):
        return (self.at(0, 1), self.at(0, -1), self.at(1, 0), self.at(0, 0, 1 - self.c))


def greet(partners):
    barrier = pltpu.get_barrier_semaphore()
    for partner in partners:
        pl.semaphore_signal(barrier, inc=1, device_id={"tp": partner}, device_id_type=MESH)
    pl.semaphore_wait(barrier, len(partners))


def greet_all(place, count):
    barrier = pltpu.get_barrier_semaphore()

    def one(j, carry):
        pl.semaphore_signal(
            barrier, inc=1, device_id={"tp": lax.rem(place.t + j, count)}, device_id_type=MESH
        )
        return carry

    lax.fori_loop(1, count, one, 0)
    pl.semaphore_wait(barrier, count - 1)


def remote(src, dst, send_sem, recv_sem, target):
    return pltpu.make_async_remote_copy(
        src_ref=src,
        dst_ref=dst,
        send_sem=send_sem,
        recv_sem=recv_sem,
        device_id={"tp": target},
        device_id_type=MESH,
    )


def gather_sems():
    dma = pltpu.SemaphoreType.DMA
    return [dma((3, 8)), dma((3, 8)), dma((9,)), dma((9,)), dma((4, 8)), dma((4, 8))]


def gather_rows(place, low, high, sems):
    z_send, z_recv, x_send, x_recv, c_send, c_recv = sems
    streams = ((low, 0), (low, 1), (high, 0))
    sibling = place.at(0, 0, 1 - place.c)
    across = place.at(1, 0)
    sent = []

    def start(copy):
        copy.start()
        sent.append(copy)

    def ring_copy(s, slot, block, target):
        ref = streams[s][0]
        return remote(ref.at[block], ref.at[block], z_send.at[s, slot], z_recv.at[s, slot], target)

    def ring_send(s, offset, direction):
        landed = offset - direction
        slot = OFFSETS.index(4 if landed == -4 else landed)
        block = place.at(streams[s][1], offset)
        start(ring_copy(s, slot, block, place.at(0, direction)))

    def ring_wait(s, slot):
        block = place.at(streams[s][1], OFFSETS[slot])
        ring_copy(s, slot, block, place.at(0, 1)).wait_recv()

    def across_copy(slot, ref, block):
        return remote(ref.at[block], ref.at[block], x_send.at[slot], x_recv.at[slot], across)

    def to_sibling(ref, row, slot):
        q = (0 if ref is low else 2) + row
        block = place.at(row, OFFSETS[slot])
        over = MIRROR[slot]
        start(
            remote(ref.at[block], ref.at[block], c_send.at[q, over], c_recv.at[q, over], sibling)
        )

    mine = place.t
    start(across_copy(8, low, mine))
    for s in (0, 2):
        for direction in (1, -1):
            ring_send(s, 0, direction)
    start(across_copy(0, high, mine))
    to_sibling(low, 0, 0)
    to_sibling(high, 0, 0)
    across_copy(8, low, across).wait_recv()
    for direction in (1, -1):
        ring_send(1, 0, direction)
    to_sibling(low, 1, 0)
    for level in range(1, 5):
        for s in (0, 2, 1):
            ref, row = streams[s]
            for slot in LEVELS[level]:
                ring_wait(s, slot)
                offset = OFFSETS[slot]
                direction = -1 if offset > 0 else 1
                if level < 3 or (level == 3 and direction == (-1 if s == 1 else 1)):
                    ring_send(s, offset, direction)
                if s == 2:
                    block = place.at(0, offset)
                    start(across_copy(slot, high, block))
                to_sibling(ref, row, slot)
        for slot in LEVELS[level - 1]:
            across_copy(slot, high, place.at(1, OFFSETS[slot])).wait_recv()
            to_sibling(high, 1, slot)
    for slot in LEVELS[4]:
        across_copy(slot, high, place.at(1, OFFSETS[slot])).wait_recv()
        to_sibling(high, 1, slot)
    for slot in range(8):
        for q in range(4):
            ref, row = (low if q < 2 else high), q % 2
            block = place.at(row, OFFSETS[slot], 1 - place.c)
            remote(
                ref.at[block], ref.at[block], c_send.at[q, slot], c_recv.at[q, slot], sibling
            ).wait_recv()
    for copy in sent:
        copy.wait_send()


def scatter_scratch(rows, width):
    low = split_of(width)
    high = width - low
    dma = pltpu.SemaphoreType.DMA
    half = jnp.bfloat16
    return [
        pltpu.VMEM((2, 8, rows, width), half),
        pltpu.VMEM((8, rows, high), half),
        pltpu.VMEM((8, rows, high), half),
        pltpu.VMEM((2, 8, rows, low), half),
        pltpu.VMEM((2, 8, rows, low), half),
        pltpu.VMEM((8, rows, high), half),
        pltpu.VMEM((8, rows, high), half),
        pltpu.VMEM((2, rows, low), half),
        dma((2, 8)),
        dma((2, 8)),
        dma((9,)),
        dma((9,)),
        dma((3, 8)),
        dma((3, 8)),
    ]


def scatter_sums(place, terms, scratch):
    (
        other, high_out, high_in, low_ring_out, low_ring_in, high_ring_out, high_ring_in, last,
        c_send, c_recv, x_send, x_recv, z_send, z_recv,
    ) = scratch
    low = low_ring_out.shape[-1]
    width = terms.shape[-1]
    sibling = place.at(0, 0, 1 - place.c)
    across = place.at(1, 0)
    sent = []
    f32 = jnp.float32

    def start(copy):
        copy.start()
        sent.append(copy)

    def core_copy(row, slot, over):
        block = place.at(row, OFFSETS[slot], 1 - place.c)
        return remote(
            terms.at[block], other.at[row, over], c_send.at[row, over], c_recv.at[row, over], sibling
        )

    for level in (4, 3, 2, 1, 0):
        for slot in LEVELS[level]:
            for row in (1, 0):
                start(core_copy(row, slot, MIRROR[slot]))

    have = set()

    def chip_term(row, slot, first, last_col):
        if (row, slot) not in have:
            core_copy(row, slot, slot).wait_recv()
            have.add((row, slot))
        block = place.at(row, OFFSETS[slot])
        own = terms[block, :, first:last_col].astype(f32)
        return own + other[row, slot, :, first:last_col].astype(f32)

    def across_copy(slot):
        return remote(high_out.at[slot], high_in.at[slot], x_send.at[slot], x_recv.at[slot], across)

    def send_across(level):
        for slot in LEVELS[level]:
            high_out[slot] = chip_term(1, slot, low, width).astype(jnp.bfloat16)
            start(across_copy(slot))

    def ring_bufs(s):
        if s == 2:
            return high_ring_out, high_ring_in
        return low_ring_out.at[s], low_ring_in.at[s]

    def ring_copy(s, slot, landing, target):
        out, landed = ring_bufs(s)
        return remote(
            out.at[slot], landed.at[landing], z_send.at[s, slot], z_recv.at[s, landing], target
        )

    def landing_of(direction, distance):
        if distance == 0:
            return 0 if direction == 1 else 7
        return OFFSETS.index(direction * distance)

    def local_term(s, slot):
        if s == 2:
            value = chip_term(0, slot, low, width)
            across_copy(slot).wait_recv()
            return value + high_in[slot].astype(f32)
        return chip_term(s, slot, 0, low)

    def arrived(s, landing):
        ring_copy(s, 0, landing, place.at(0, 1)).wait_recv()
        return ring_bufs(s)[1][landing].astype(f32)

    def ring_level(s, level):
        long_way = -1 if s == 1 else 1
        for slot in LEVELS[level]:
            if level == 4:
                direction = long_way
            else:
                direction = 1 if OFFSETS[slot] > 0 else -1
            value = local_term(s, slot)
            if level < 3 or (level == 3 and direction == long_way):
                value = value + arrived(s, landing_of(direction, level))
            ring_bufs(s)[0][slot] = value.astype(jnp.bfloat16)
            start(ring_copy(s, slot, landing_of(direction, level - 1), place.at(0, direction)))

    def ring_end(s):
        value = local_term(s, 0)
        for direction in (1, -1):
            value = value + arrived(s, landing_of(direction, 0))
        return value

    send_across(4)
    send_across(3)
    for level in (4, 3, 2, 1):
        if level >= 2:
            send_across(level - 2)
        for s in (1, 0, 2):
            ring_level(s, level)
    last[0] = ring_end(1).astype(jnp.bfloat16)
    end = remote(last.at[0], last.at[1], x_send.at[8], x_recv.at[8], across)
    start(end)
    low_sum = ring_end(0)
    high_sum = ring_end(2)
    end.wait_recv()
    low_sum = low_sum + last[1].astype(f32)
    for copy in sent:
        copy.wait_send()
    return low_sum, high_sum


def swap_blocks(place, src, dst, send_sem, recv_sem, count):
    def copy(j):
        target = lax.rem(place.t + j, count)
        return remote(src.at[target], dst.at[place.t], send_sem.at[j], recv_sem.at[j], target)

    def begin(j, carry):
        copy(j).start()
        return carry

    def end(j, carry):
        source = lax.rem(place.t - j + count, count)
        remote(
            src.at[source], dst.at[source], send_sem.at[j], recv_sem.at[j], source
        ).wait_recv()
        copy(j).wait_send()
        return carry

    lax.fori_loop(1, count, begin, 0)
    lax.fori_loop(1, count, end, 0)


def normalise(low, high, gain, width):
    cut = low.shape[-1]
    total = jnp.sum(low * low, axis=-1, keepdims=True) + jnp.sum(high * high, axis=-1, keepdims=True)
    scale = lax.rsqrt(total / width + EPSILON)
    return (
        (low * scale * gain[:, :cut]).astype(jnp.bfloat16),
        (high * scale * gain[:, cut:]).astype(jnp.bfloat16),
    )


def vmem():
    return pl.BlockSpec(memory_space=pltpu.VMEM)


def params(identity):
    return pltpu.CompilerParams(
        collective_id=identity, has_side_effects=True, vmem_limit_bytes=60 * 2**20
    )


def project_kernel(
    count, hidden, gain, w_query, w_keyval, out, low, high, projected, landed, *sems
):
    place = Place()
    greet_all(place, count)
    rows, width = hidden.shape
    cut = low.shape[-1]
    values = hidden[...].astype(jnp.float32)
    first, second = normalise(values[:, :cut], values[:, cut:], gain[...], width)
    low[place.t] = first
    high[place.t] = second
    gather_rows(place, low, high, sems[:6])
    parts = 4
    blocks = count // parts
    for part in range(parts):
        span = slice(part * blocks, (part + 1) * blocks)
        low_rows = low[span].reshape(blocks * rows, cut)
        high_rows = high[span].reshape(blocks * rows, width - cut)
        start = 0
        for weights in (w_query, w_keyval):
            columns = weights.shape[1]
            value = jnp.dot(low_rows, weights[:cut], preferred_element_type=jnp.float32)
            value += jnp.dot(high_rows, weights[cut:], preferred_element_type=jnp.float32)
            projected[span, :, start : start + columns] = value.astype(jnp.bfloat16).reshape(
                blocks, rows, columns
            )
            start += columns
    landed[place.t] = projected[place.t]
    swap_blocks(place, projected, landed, sems[6], sems[7], count)
    out[...] = landed[...]


def project(hidden, gain, w_query, w_keyval, count):
    rows, width = hidden.shape
    cut = split_of(width)
    columns = w_query.shape[1] + w_keyval.shape[1]
    dma = pltpu.SemaphoreType.DMA
    half = jnp.bfloat16
    return pl.pallas_call(
        functools.partial(project_kernel, count),
        out_shape=jax.ShapeDtypeStruct((count, rows, columns), half),
        in_specs=[vmem()] * 4,
        out_specs=vmem(),
        scratch_shapes=[
            pltpu.VMEM((count, rows, cut), half),
            pltpu.VMEM((count, rows, width - cut), half),
            pltpu.VMEM((count, rows, columns), half),
            pltpu.VMEM((count, rows, columns), half),
        ]
        + gather_sems()
        + [dma((count,)), dma((count,))],
        compiler_params=params(0),
        name="project",
    )(hidden, gain.reshape(1, width), w_query, w_keyval)


def combine_kernel(
    count, attended, hidden, gain, w_out, middle, low_out, high_out, landed, terms, low, high, *rest
):
    place = Place()
    greet_all(place, count)
    rows, width = hidden.shape
    cut = low.shape[-1]
    swap_send, swap_recv, out_sem = rest[:3]
    landed[place.t] = attended[place.t]
    swap_blocks(place, attended, landed, swap_send, swap_recv, count)
    parts = 4
    blocks = count // parts
    for part in range(parts):
        span = slice(part * blocks, (part + 1) * blocks)
        heads = landed[span].reshape(blocks * rows, landed.shape[-1])
        terms[span] = (
            jnp.dot(heads, w_out[...], preferred_element_type=jnp.float32)
            .astype(jnp.bfloat16)
            .reshape(blocks, rows, width)
        )
    low_sum, high_sum = scatter_sums(place, terms, rest[9:])
    values = hidden[...].astype(jnp.float32)
    low_mid = (values[:, :cut] + low_sum).astype(jnp.bfloat16)
    high_mid = (values[:, cut:] + high_sum).astype(jnp.bfloat16)
    middle[:, :cut] = low_mid
    middle[:, cut:] = high_mid
    first, second = normalise(
        low_mid.astype(jnp.float32), high_mid.astype(jnp.float32), gain[...], width
    )
    low[place.t] = first
    high[place.t] = second
    gather_rows(place, low, high, rest[3:9])
    copies = [
        pltpu.make_async_copy(low, low_out, out_sem.at[0]),
        pltpu.make_async_copy(high, high_out, out_sem.at[1]),
    ]
    for copy in copies:
        copy.start()
    for copy in copies:
        copy.wait()


def combine(attended, hidden, gain, w_out, count):
    rows, width = hidden.shape
    cut = split_of(width)
    dma = pltpu.SemaphoreType.DMA
    half = jnp.bfloat16
    return pl.pallas_call(
        functools.partial(combine_kernel, count),
        out_shape=(
            jax.ShapeDtypeStruct((rows, width), half),
            jax.ShapeDtypeStruct((count, rows, cut), half),
            jax.ShapeDtypeStruct((count, rows, width - cut), half),
        ),
        in_specs=[vmem()] * 4,
        out_specs=(vmem(), pl.BlockSpec(memory_space=pl.ANY), pl.BlockSpec(memory_space=pl.ANY)),
        scratch_shapes=[
            pltpu.VMEM(attended.shape, half),
            pltpu.VMEM((count, rows, width), half),
            pltpu.VMEM((count, rows, cut), half),
            pltpu.VMEM((count, rows, width - cut), half),
            dma((count,)),
            dma((count,)),
            dma((2,)),
        ]
        + gather_sems()
        + scatter_scratch(rows, width),
        compiler_params=params(1),
        name="combine",
    )(attended, hidden, gain.reshape(1, width), w_out)


def finish_kernel(terms, middle, out, *scratch):
    place = Place()
    greet(place.neighbours())
    cut = split_of(middle.shape[-1])
    low_sum, high_sum = scatter_sums(place, terms, scratch)
    values = middle[...].astype(jnp.float32)
    out[:, :cut] = (values[:, :cut] + low_sum).astype(jnp.bfloat16)
    out[:, cut:] = (values[:, cut:] + high_sum).astype(jnp.bfloat16)


def finish_layer(terms, middle):
    rows, width = middle.shape
    return pl.pallas_call(
        finish_kernel,
        out_shape=jax.ShapeDtypeStruct((rows, width), jnp.bfloat16),
        in_specs=[vmem()] * 2,
        out_specs=vmem(),
        scratch_shapes=scatter_scratch(rows, width),
        compiler_params=params(2),
        name="finish_layer",
    )(terms, middle)


def tree_paths(parent_row, depth_limit):
    count = parent_row.shape[0]
    identity = jnp.eye(count, dtype=jnp.bool_)
    ancestry = identity
    for level in range(depth_limit):
        ancestry = identity | jnp.take(ancestry, parent_row, axis=0)
    depths = jnp.sum(ancestry.astype(jnp.int32), axis=1) - 1
    return (ancestry, depths)


def rotate(values, positions):
    half = values.shape[-1] // 2
    steps_f = jnp.arange(half).astype(jnp.float32)
    inverse = jnp.exp(steps_f * (-2.0 * math.log(THETA) / values.shape[-1]))
    angles = positions[:, None] * inverse[None, :]
    cosine = jnp.cos(angles)[:, None, :]
    sine = jnp.sin(angles)[:, None, :]
    first = values[..., :half].astype(jnp.float32)
    second = values[..., half:].astype(jnp.float32)
    turned = jnp.concatenate(
        [first * cosine - second * sine, second * cosine + first * sine], axis=-1
    )
    return turned.astype(jnp.bfloat16)


def prepare(query, keyval, length, parent_row, depth_limit):
    draft, heads, head_dim = query.shape
    kv_width = keyval.shape[1] // 2
    kv_heads = kv_width // head_dim
    ancestry, depths = tree_paths(parent_row, depth_limit)
    positions = (length + depths).astype(jnp.float32)
    query_rot = rotate(query, positions)
    new_keys = rotate(keyval[:, :kv_width].reshape(draft, kv_heads, head_dim), positions)
    new_values = keyval[:, kv_width:].reshape(draft, kv_heads, head_dim)
    grouped = query_rot.reshape(draft, kv_heads, heads // kv_heads, head_dim)
    draft_scores = jnp.einsum(
        "jgqd,kgd->gqjk", grouped, new_keys, preferred_element_type=jnp.float32
    ) * (1.0 / math.sqrt(head_dim))
    draft_scores = jnp.where(ancestry[None, None], draft_scores, -jnp.inf)
    return (grouped, new_keys, new_values, ancestry, depths, draft_scores)


def accept_rows(new_keys, new_values, ancestry, depths, leaf, depth_limit):
    draft = depths.shape[0]
    selector = ancestry[leaf][None, :] & (depths[None, :] == jnp.arange(depth_limit)[:, None])
    new_rows = jnp.concatenate([new_keys.reshape(draft, -1), new_values.reshape(draft, -1)], axis=1)
    return jnp.dot(
        selector.astype(jnp.bfloat16), new_rows, preferred_element_type=jnp.float32
    ).astype(jnp.bfloat16)


def finish(weighted, total, draft):
    return (
        (weighted / jnp.transpose(total, (2, 0, 1))[..., None])
        .astype(jnp.bfloat16)
        .reshape(draft, -1)
    )


def attend_padded(query, keyval, keys_cache, values_cache, length, parent_row, leaf, depth_limit):
    draft, heads, head_dim = query.shape
    grouped, new_keys, new_values, ancestry, depths, draft_scores = prepare(
        query, keyval, length, parent_row, depth_limit
    )
    slots = keys_cache.shape[0]
    kv_heads = new_keys.shape[1]
    cache_k = keys_cache.reshape(slots, kv_heads, head_dim)
    cache_v = values_cache.reshape(slots, kv_heads, head_dim)
    cache_scores = jnp.einsum(
        "jgqd,pgd->gqjp", grouped, cache_k, preferred_element_type=jnp.float32
    ) * (1.0 / math.sqrt(head_dim))
    live = jnp.arange(slots) < length
    cache_scores = jnp.where(live[None, None, None], cache_scores, -jnp.inf)
    top = jnp.maximum(jnp.max(draft_scores, axis=-1), jnp.max(cache_scores, axis=-1))
    draft_exp = jnp.exp(draft_scores - top[..., None])
    cache_exp = jnp.exp(cache_scores - top[..., None])
    total = jnp.sum(draft_exp, axis=-1) + jnp.sum(cache_exp, axis=-1)
    weighted = jnp.einsum(
        "gqjk,kgd->jgqd",
        draft_exp.astype(jnp.bfloat16),
        new_values,
        preferred_element_type=jnp.float32,
    )
    weighted = weighted + jnp.einsum(
        "gqjp,pgd->jgqd",
        cache_exp.astype(jnp.bfloat16),
        cache_v,
        preferred_element_type=jnp.float32,
    )
    return (
        finish(weighted, total, draft),
        accept_rows(new_keys, new_values, ancestry, depths, leaf, depth_limit),
    )


def gate_weights(inputs, router, routes):
    logits = jnp.dot(inputs, router, preferred_element_type=jnp.float32)
    onehot = routes[:, :, None] == jnp.arange(router.shape[1])[None, None, :]
    picked = jnp.sum(jnp.where(onehot, logits[:, None, :], 0.0), axis=2)
    return jax.nn.softmax(picked, axis=1).astype(jnp.bfloat16)


def expert_slots(inputs, weights, routes, expert, gate_rows, up_rows, down_rows, capacity):
    count = inputs.shape[0]
    match = routes == expert
    hits = jnp.any(match, axis=1)
    gate_of = jnp.sum(jnp.where(match, weights.astype(jnp.float32), 0.0), axis=1)
    slot_ids = jnp.cumsum(hits.astype(jnp.int32)) - 1
    target = jnp.where(hits, slot_ids, capacity)
    index = jnp.full((capacity,), count, jnp.int32).at[target].set(jnp.arange(count), mode="drop")
    valid = index < count
    safe = jnp.minimum(index, count - 1)
    picked = inputs[safe]
    gate_val = lax.dot_general(
        picked, gate_rows, (((1,), (1,)), ((), ())), preferred_element_type=jnp.float32
    )
    up_val = lax.dot_general(
        picked, up_rows, (((1,), (1,)), ((), ())), preferred_element_type=jnp.float32
    )
    active = (gate_val * jax.nn.sigmoid(SWIGLU_ALPHA * gate_val) * (up_val + 1.0)).astype(
        jnp.bfloat16
    )
    result = jnp.dot(active, down_rows, preferred_element_type=jnp.float32)
    scale_rows = jnp.where(valid, gate_of[safe], 0.0)
    return (result * scale_rows[:, None], index)


def local(
    hidden,
    attn_gain,
    w_query,
    w_keyval,
    w_out,
    cache_keys,
    cache_values,
    cache_lens,
    parents,
    accepted,
    moe_gain,
    w_router,
    routes,
    w_gate,
    w_up,
    w_down,
):
    devices = lax.axis_size("tp")
    index_me = lax.axis_index("tp")
    rows = hidden.shape[0]
    local_query = w_query.shape[1]
    projected = project(hidden, attn_gain, w_query, w_keyval, devices)
    width = projected.shape[2]
    gathered_cols = jnp.transpose(projected, (1, 0, 2))
    requests = cache_lens.shape[0]
    draft = parents.shape[1]
    query = gathered_cols[:, :, :local_query].reshape(requests, draft, HEADS, HEAD_DIM)
    keyval = gathered_cols[:, :, local_query:].reshape(
        requests, draft, devices * (width - local_query)
    )

    def per_request(items):
        return attend_padded(*items, DEPTH)

    attended, accepted_kv = lax.map(
        per_request, (query, keyval, cache_keys, cache_values, cache_lens, parents, accepted)
    )
    attended = jnp.transpose(attended.reshape(rows, devices, local_query), (1, 0, 2))
    middle, low, high = combine(attended, hidden, moe_gain, w_out, devices)
    count = devices * rows
    all_inputs = jnp.concatenate([low, high], axis=2).reshape(count, hidden.shape[1])
    all_weights = gate_weights(all_inputs, w_router, routes)
    units = w_down.shape[0]
    expert = index_me * units // EXPERT_HID
    capacity = 2 * count * routes.shape[1] // w_router.shape[1]
    slot_rows, slot_index = expert_slots(
        all_inputs, all_weights, routes, expert, w_gate, w_up, w_down, capacity
    )
    term = (
        jnp.zeros((count, all_inputs.shape[1]), jnp.float32)
        .at[slot_index]
        .add(slot_rows, mode="drop")
    )
    layer_out = finish_layer(
        term.astype(jnp.bfloat16).reshape(devices, rows, all_inputs.shape[1]), middle
    )
    return (layer_out, accepted_kv)


def solution(mesh):
    return jax.shard_map(
        local,
        mesh=mesh,
        in_specs=(
            P(("dp", "tp"), None),
            P(),
            P(None, "tp"),
            P(None, "tp"),
            P("tp", None),
            P(("dp", "tp"), None, None),
            P(("dp", "tp"), None, None),
            P(("dp", "tp")),
            P(("dp", "tp"), None),
            P(("dp", "tp")),
            P(),
            P(),
            P("dp", None),
            P("tp", None),
            P("tp", None),
            P("tp", None),
        ),
        out_specs=(P(("dp", "tp"), None), P(("dp", "tp"), None, None)),
        check_vma=False,
    )
```

```python
import functools
import math

import jax
import jax.numpy as jnp
from jax import lax
from jax.experimental import pallas as pl
from jax.experimental.pallas import tpu as pltpu
from jax.sharding import PartitionSpec as P

HEADS = 64
HEAD_DIM = 64
EXPERT_HID = 2880
DEPTH = 8


THETA = 150000.0
SWIGLU_ALPHA = 1.702
EPSILON = 1e-05

MESH = pl.DeviceIdType.MESH
RING = 8
OFFSETS = (0, 1, -1, 2, -2, 3, -3, 4)
MIRROR = (0, 2, 1, 4, 3, 6, 5, 7)
LEVELS = ((0,), (1, 2), (3, 4), (5, 6), (7,))


def split_of(width):
    return (width // 2) // 128 * 128


class Place:
    def __init__(self):
        self.t = lax.axis_index("tp")
        self.c = lax.rem(self.t, 2)
        self.z = lax.rem(self.t // 2, RING)
        self.x = self.t // (2 * RING)
        self.forward = 1 - 2 * self.c

    def at(self, row, offset, core=None):
        z = lax.rem(self.z + self.forward * offset + 2 * RING, RING)
        x = self.x if row == 0 else 1 - self.x
        return (x * RING + z) * 2 + (self.c if core is None else core)

    def blocks(self, level):
        return [
            self.at(row, OFFSETS[slot], core)
            for slot in LEVELS[level]
            for row in (0, 1)
            for core in (self.c, 1 - self.c)
        ]


def greet_all(place, count):
    barrier = pltpu.get_barrier_semaphore()

    def one(j, carry):
        pl.semaphore_signal(
            barrier, inc=1, device_id={"tp": lax.rem(place.t + j, count)}, device_id_type=MESH
        )
        return carry

    lax.fori_loop(1, count, one, 0)
    pl.semaphore_wait(barrier, count - 1)


def remote(src, dst, send_sem, recv_sem, target):
    return pltpu.make_async_remote_copy(
        src_ref=src,
        dst_ref=dst,
        send_sem=send_sem,
        recv_sem=recv_sem,
        device_id={"tp": target},
        device_id_type=MESH,
    )


def gather_sems():
    dma = pltpu.SemaphoreType.DMA
    return [dma((3, 8)), dma((3, 8)), dma((9,)), dma((9,)), dma((4, 8)), dma((4, 8))]


def gather_rows(place, low, high, sems, work):
    z_send, z_recv, x_send, x_recv, c_send, c_recv = sems
    streams = ((low, 0), (low, 1), (high, 0))
    sibling = place.at(0, 0, 1 - place.c)
    across = place.at(1, 0)
    sent = []

    def start(copy):
        copy.start()
        sent.append(copy)

    def ring_copy(s, slot, block, target):
        ref = streams[s][0]
        return remote(ref.at[block], ref.at[block], z_send.at[s, slot], z_recv.at[s, slot], target)

    def ring_send(s, offset, direction):
        landed = offset - direction
        slot = OFFSETS.index(4 if landed == -4 else landed)
        block = place.at(streams[s][1], offset)
        start(ring_copy(s, slot, block, place.at(0, direction)))

    def ring_wait(s, slot):
        block = place.at(streams[s][1], OFFSETS[slot])
        ring_copy(s, slot, block, place.at(0, 1)).wait_recv()

    def across_copy(slot, ref, block):
        return remote(ref.at[block], ref.at[block], x_send.at[slot], x_recv.at[slot], across)

    def to_sibling(ref, row, slot):
        q = (0 if ref is low else 2) + row
        block = place.at(row, OFFSETS[slot])
        over = MIRROR[slot]
        start(
            remote(ref.at[block], ref.at[block], c_send.at[q, over], c_recv.at[q, over], sibling)
        )

    def settle(level):
        for slot in LEVELS[level]:
            across_copy(slot, high, place.at(1, OFFSETS[slot])).wait_recv()
            to_sibling(high, 1, slot)
        for slot in LEVELS[level]:
            for q in range(4):
                ref, row = (low if q < 2 else high), q % 2
                block = place.at(row, OFFSETS[slot], 1 - place.c)
                remote(
                    ref.at[block], ref.at[block], c_send.at[q, slot], c_recv.at[q, slot], sibling
                ).wait_recv()
        work(level)

    mine = place.t
    start(across_copy(8, low, mine))
    for s in (0, 2):
        for direction in (1, -1):
            ring_send(s, 0, direction)
    start(across_copy(0, high, mine))
    to_sibling(low, 0, 0)
    to_sibling(high, 0, 0)
    across_copy(8, low, across).wait_recv()
    for direction in (1, -1):
        ring_send(1, 0, direction)
    to_sibling(low, 1, 0)
    for level in range(1, 5):
        for s in (0, 2, 1):
            ref, row = streams[s]
            for slot in LEVELS[level]:
                ring_wait(s, slot)
                offset = OFFSETS[slot]
                direction = -1 if offset > 0 else 1
                if level < 3 or (level == 3 and direction == (-1 if s == 1 else 1)):
                    ring_send(s, offset, direction)
                if s == 2:
                    block = place.at(0, offset)
                    start(across_copy(slot, high, block))
                to_sibling(ref, row, slot)
        settle(level - 1)
    settle(4)
    for copy in sent:
        copy.wait_send()


def scatter_scratch(rows, width):
    low = split_of(width)
    high = width - low
    dma = pltpu.SemaphoreType.DMA
    half = jnp.bfloat16
    return [
        pltpu.VMEM((2, 8, rows, width), half),
        pltpu.VMEM((8, rows, high), half),
        pltpu.VMEM((8, rows, high), half),
        pltpu.VMEM((2, 8, rows, low), half),
        pltpu.VMEM((2, 8, rows, low), half),
        pltpu.VMEM((8, rows, high), half),
        pltpu.VMEM((8, rows, high), half),
        pltpu.VMEM((2, rows, low), half),
        dma((2, 8)),
        dma((2, 8)),
        dma((9,)),
        dma((9,)),
        dma((3, 8)),
        dma((3, 8)),
    ]


def core_term(place, terms, scratch, row, slot, over):
    other, c_send, c_recv = scratch[0], scratch[8], scratch[9]
    sibling = place.at(0, 0, 1 - place.c)
    block = place.at(row, OFFSETS[slot], 1 - place.c)
    return remote(
        terms.at[block], other.at[row, over], c_send.at[row, over], c_recv.at[row, over], sibling
    )


def core_terms(place, terms, scratch, level):
    copies = [
        core_term(place, terms, scratch, row, slot, MIRROR[slot])
        for slot in LEVELS[level]
        for row in (1, 0)
    ]
    for copy in copies:
        copy.start()
    return copies


def scatter_sums(place, terms, scratch, core_sent):
    (
        other, high_out, high_in, low_ring_out, low_ring_in, high_ring_out, high_ring_in, last,
        _, _, x_send, x_recv, z_send, z_recv,
    ) = scratch
    low = low_ring_out.shape[-1]
    width = terms.shape[-1]
    across = place.at(1, 0)
    sent = []
    f32 = jnp.float32

    def start(copy):
        copy.start()
        sent.append(copy)

    def core_copy(row, slot, over):
        return core_term(place, terms, scratch, row, slot, over)

    sent.extend(core_sent)
    have = set()

    def chip_term(row, slot, first, last_col):
        if (row, slot) not in have:
            core_copy(row, slot, slot).wait_recv()
            have.add((row, slot))
        block = place.at(row, OFFSETS[slot])
        own = terms[block, :, first:last_col].astype(f32)
        return own + other[row, slot, :, first:last_col].astype(f32)

    def across_copy(slot):
        return remote(high_out.at[slot], high_in.at[slot], x_send.at[slot], x_recv.at[slot], across)

    def send_across(level):
        for slot in LEVELS[level]:
            high_out[slot] = chip_term(1, slot, low, width).astype(jnp.bfloat16)
            start(across_copy(slot))

    def ring_bufs(s):
        if s == 2:
            return high_ring_out, high_ring_in
        return low_ring_out.at[s], low_ring_in.at[s]

    def ring_copy(s, slot, landing, target):
        out, landed = ring_bufs(s)
        return remote(
            out.at[slot], landed.at[landing], z_send.at[s, slot], z_recv.at[s, landing], target
        )

    def landing_of(direction, distance):
        if distance == 0:
            return 0 if direction == 1 else 7
        return OFFSETS.index(direction * distance)

    def local_term(s, slot):
        if s == 2:
            value = chip_term(0, slot, low, width)
            across_copy(slot).wait_recv()
            return value + high_in[slot].astype(f32)
        return chip_term(s, slot, 0, low)

    def arrived(s, landing):
        ring_copy(s, 0, landing, place.at(0, 1)).wait_recv()
        return ring_bufs(s)[1][landing].astype(f32)

    def ring_level(s, level):
        long_way = -1 if s == 1 else 1
        for slot in LEVELS[level]:
            if level == 4:
                direction = long_way
            else:
                direction = 1 if OFFSETS[slot] > 0 else -1
            value = local_term(s, slot)
            if level < 3 or (level == 3 and direction == long_way):
                value = value + arrived(s, landing_of(direction, level))
            ring_bufs(s)[0][slot] = value.astype(jnp.bfloat16)
            start(ring_copy(s, slot, landing_of(direction, level - 1), place.at(0, direction)))

    def ring_end(s):
        value = local_term(s, 0)
        for direction in (1, -1):
            value = value + arrived(s, landing_of(direction, 0))
        return value

    send_across(4)
    send_across(3)
    for level in (4, 3, 2, 1):
        if level >= 2:
            send_across(level - 2)
        for s in (1, 0, 2):
            ring_level(s, level)
    last[0] = ring_end(1).astype(jnp.bfloat16)
    end = remote(last.at[0], last.at[1], x_send.at[8], x_recv.at[8], across)
    start(end)
    low_sum = ring_end(0)
    high_sum = ring_end(2)
    end.wait_recv()
    low_sum = low_sum + last[1].astype(f32)
    for copy in sent:
        copy.wait_send()
    return low_sum, high_sum


def swap_send(place, src, dst, send_sem, recv_sem, level):
    copies = []
    for block in place.blocks(level):
        if level == 0 and not copies:
            copies.append(None)
            continue
        copy = remote(
            src.at[block], dst.at[place.t], send_sem.at[block], recv_sem.at[place.t], block
        )
        copy.start()
        copies.append(copy)
    return [copy for copy in copies if copy is not None]


def swap_wait(place, src, dst, send_sem, recv_sem, level):
    for i, block in enumerate(place.blocks(level)):
        if level == 0 and i == 0:
            continue
        remote(
            src.at[block], dst.at[block], send_sem.at[block], recv_sem.at[block], block
        ).wait_recv()


def normalise(low, high, gain, width):
    cut = low.shape[-1]
    total = jnp.sum(low * low, axis=-1, keepdims=True) + jnp.sum(high * high, axis=-1, keepdims=True)
    scale = lax.rsqrt(total / width + EPSILON)
    return (
        (low * scale * gain[:, :cut]).astype(jnp.bfloat16),
        (high * scale * gain[:, cut:]).astype(jnp.bfloat16),
    )


def vmem():
    return pl.BlockSpec(memory_space=pltpu.VMEM)


def in_place():
    return pl.BlockSpec(memory_space=pl.ANY)


def params(identity):
    return pltpu.CompilerParams(
        collective_id=identity, has_side_effects=True, vmem_limit_bytes=60 * 2**20
    )


def dot_rows(a, b):
    return lax.dot_general(a, b, (((1,), (1,)), ((), ())), preferred_element_type=jnp.float32)


def stage(buffer, ref, blocks):
    for i, block in enumerate(blocks):
        buffer[i] = ref[block]
    value = buffer[: len(blocks)]
    return value.reshape(len(blocks) * value.shape[1], value.shape[2])


def project_kernel(
    count, hidden, gain, w_query, w_keyval, out,
    low, high, projected, landed, stage_low, stage_high, swap_out, swap_in, *sems
):
    place = Place()
    greet_all(place, count)
    rows, width = hidden.shape
    cut = low.shape[-1]
    values = hidden[...].astype(jnp.float32)
    first, second = normalise(values[:, :cut], values[:, cut:], gain[...], width)
    low[place.t] = first
    high[place.t] = second
    sent = []
    split = w_query.shape[1]

    def work(level):
        blocks = place.blocks(level)
        low_rows = stage(stage_low, low, blocks)
        high_rows = stage(stage_high, high, blocks)
        query = jnp.dot(low_rows, w_query[:cut], preferred_element_type=jnp.float32)
        query += jnp.dot(high_rows, w_query[cut:], preferred_element_type=jnp.float32)
        keyval = dot_rows(low_rows, w_keyval[:, :cut]) + dot_rows(high_rows, w_keyval[:, cut:])
        query = query.astype(jnp.bfloat16).reshape(len(blocks), rows, split)
        keyval = keyval.astype(jnp.bfloat16).reshape(len(blocks), rows, w_keyval.shape[0])
        for i, block in enumerate(blocks):
            projected[block, :, :split] = query[i]
            projected[block, :, split:] = keyval[i]
        sent.extend(swap_send(place, projected, landed, swap_out, swap_in, level))

    gather_rows(place, low, high, sems, work)
    landed[place.t] = projected[place.t]
    for level in range(5):
        swap_wait(place, projected, landed, swap_out, swap_in, level)
    for copy in sent:
        copy.wait_send()
    out[...] = landed[...]


def project(hidden, gain, w_query, w_keyval, count):
    rows, width = hidden.shape
    cut = split_of(width)
    columns = w_query.shape[1] + w_keyval.shape[0]
    dma = pltpu.SemaphoreType.DMA
    half = jnp.bfloat16
    return pl.pallas_call(
        functools.partial(project_kernel, count),
        out_shape=jax.ShapeDtypeStruct((count, rows, columns), half),
        in_specs=[vmem()] * 4,
        out_specs=vmem(),
        scratch_shapes=[
            pltpu.VMEM((count, rows, cut), half),
            pltpu.VMEM((count, rows, width - cut), half),
            pltpu.VMEM((count, rows, columns), half),
            pltpu.VMEM((count, rows, columns), half),
            pltpu.VMEM((8, rows, cut), half),
            pltpu.VMEM((8, rows, width - cut), half),
            dma((count,)),
            dma((count,)),
        ]
        + gather_sems(),
        compiler_params=params(0),
        name="project",
    )(hidden, gain.reshape(1, width), w_query, w_keyval)


def attend_kernel(
    lens, leaf, parents, blocks, keys, values, out, accepted, key_tiles, value_tiles, scores, sems
):
    f32 = jnp.float32
    half = jnp.bfloat16
    pairs = key_tiles.shape[0]
    draft = parents.shape[1]
    chunks, rows, span = scores.shape

    def loads(pair):
        columns = slice(pair * 128, (pair + 1) * 128)
        return (
            pltpu.make_async_copy(keys.at[0, :, columns], key_tiles.at[pair], sems.at[0, pair]),
            pltpu.make_async_copy(values.at[0, :, columns], value_tiles.at[pair], sems.at[1, pair]),
        )

    for pair in range(pairs):
        for copy in loads(pair):
            copy.start()
    length = lens[0]
    k_of = lax.broadcasted_iota(jnp.int32, (draft, draft), 0)
    j_of = lax.broadcasted_iota(jnp.int32, (draft, draft), 1)
    eye = (k_of == j_of).astype(half)
    is_parent = k_of == jnp.broadcast_to(parents[...], (draft, draft))
    paths = jnp.where(is_parent | (k_of == j_of), 1.0, 0.0)
    for _ in range(3):
        paths = jnp.dot(paths.astype(half), paths.astype(half), preferred_element_type=f32)
        paths = jnp.minimum(paths, 1.0)
    ancestry = lax.dot_general(
        paths.astype(half), eye, (((0,), (0,)), ((), ())), preferred_element_type=f32
    )
    depth_row = jnp.sum(paths, axis=0, keepdims=True) - 1.0
    depth = jnp.sum(ancestry, axis=1, keepdims=True) - 1.0
    positions = length.astype(f32) + depth
    lane = lax.broadcasted_iota(jnp.int32, (draft, 128), 1)
    first_half = lane % 64 < 32
    low_lanes = lane < 64
    inverse = jnp.exp((lane % 32).astype(f32) * (-2.0 * math.log(THETA) / HEAD_DIM))
    angles = positions * inverse
    cosine = jnp.cos(angles)
    sine = jnp.sin(angles)
    signed = jnp.where(first_half, -sine, sine)

    def rotated(value):
        partner = jnp.where(first_half, pltpu.roll(value, 96, 1), pltpu.roll(value, 32, 1))
        return (value * cosine + partner * signed).astype(half)

    def columns_of(first):
        return jnp.concatenate([blocks[first + q, :, 128:160].astype(f32) for q in range(4)], axis=1)

    on_path = jnp.sum(jnp.where(k_of == leaf[0], ancestry, 0.0), axis=0, keepdims=True)
    level = lax.broadcasted_iota(jnp.int32, (DEPTH, draft), 0).astype(f32)
    selector = jnp.where((on_path > 0.5) & (depth_row == level), 1.0, 0.0).astype(half)
    allowed = jnp.concatenate([ancestry] * 16, axis=0) > 0.5
    scale = 1.0 / math.sqrt(HEAD_DIM)

    for pair in range(pairs):
        new_keys = rotated(columns_of(4 * pair))
        new_values = columns_of(16 + 4 * pair).astype(half)
        columns = slice(pair * 128, (pair + 1) * 128)
        accepted[0, :, columns] = jnp.dot(selector, new_keys, preferred_element_type=f32).astype(half)
        columns = slice((4 + pair) * 128, (5 + pair) * 128)
        accepted[0, :, columns] = jnp.dot(
            selector, new_values, preferred_element_type=f32
        ).astype(half)
        lhs = []
        for i in range(8):
            turned = rotated(blocks[8 * pair + i, :, :128].astype(f32)).astype(f32) * scale
            swapped = pltpu.roll(turned, 64, 1)
            if i < 4:
                lhs.append(jnp.where(low_lanes, turned, 0.0))
                lhs.append(jnp.where(low_lanes, swapped, 0.0))
            else:
                lhs.append(jnp.where(low_lanes, 0.0, swapped))
                lhs.append(jnp.where(low_lanes, 0.0, turned))
        lhs = jnp.concatenate(lhs, axis=0).astype(half)
        draft_scores = jnp.where(allowed, dot_rows(lhs, new_keys), -jnp.inf)
        top = jnp.max(draft_scores, axis=1, keepdims=True)
        key_copy, value_copy = loads(pair)
        key_copy.wait()
        for n in range(chunks):
            part = dot_rows(lhs, key_tiles[pair, n * span : (n + 1) * span, :])
            slot = n * span + lax.broadcasted_iota(jnp.int32, (1, span), 1)
            part = jnp.where(slot < length, part, -jnp.inf)
            scores[n] = part
            top = jnp.maximum(top, jnp.max(part, axis=1, keepdims=True))
        weights = jnp.exp(draft_scores - top)
        total = jnp.sum(weights, axis=1, keepdims=True)
        weighted = jnp.dot(weights.astype(half), new_values, preferred_element_type=f32)
        value_copy.wait()
        for n in range(chunks):
            weights = jnp.exp(scores[n] - top)
            total = total + jnp.sum(weights, axis=1, keepdims=True)
            weighted = weighted + jnp.dot(
                weights.astype(half),
                value_tiles[pair, n * span : (n + 1) * span, :],
                preferred_element_type=f32,
            )
        result = weighted / total
        for i in range(8):
            even = result[2 * i * draft : (2 * i + 1) * draft]
            odd = result[(2 * i + 1) * draft : (2 * i + 2) * draft]
            if i < 4:
                both = jnp.where(low_lanes, even, pltpu.roll(odd, 64, 1))
            else:
                both = jnp.where(low_lanes, pltpu.roll(even, 64, 1), odd)
            out[8 * pair + i] = both.astype(half)


def attend(lens, leaf, parents, blocks, keys, values):
    count, draft, _ = blocks.shape
    _, slots, kv_width = keys.shape
    pairs = kv_width // 128
    chunks = 4
    half = jnp.bfloat16
    smem = pl.BlockSpec(memory_space=pltpu.SMEM)
    return pl.pallas_call(
        attend_kernel,
        out_shape=(
            jax.ShapeDtypeStruct((count, draft, 128), half),
            jax.ShapeDtypeStruct((1, DEPTH, 2 * kv_width), half),
        ),
        in_specs=[smem, smem, vmem(), vmem(), in_place(), in_place()],
        out_specs=(vmem(), vmem()),
        scratch_shapes=[
            pltpu.VMEM((pairs, slots, 128), half),
            pltpu.VMEM((pairs, slots, 128), half),
            pltpu.VMEM((chunks, 16 * draft, slots // chunks), jnp.float32),
            pltpu.SemaphoreType.DMA((2, pairs)),
        ],
        compiler_params=pltpu.CompilerParams(vmem_limit_bytes=60 * 2**20),
        name="attend",
    )(lens, leaf, parents, blocks, keys, values)


def layer_kernel(
    count, attended, hidden, gain, routes, w_router, w_out_hbm, w_gate_hbm, w_up_hbm, w_down_hbm, out,
    w_out, w_gate, w_up, w_down, weight_sems, landed, stage_heads, terms, low, high,
    stage_low, stage_high, route_cols, stage_routes, swap_out, swap_in, *rest
):
    place = Place()
    f32 = jnp.float32
    half = jnp.bfloat16
    weights = [
        pltpu.make_async_copy(source, target, weight_sems.at[i])
        for i, (source, target) in enumerate(
            ((w_out_hbm, w_out), (w_gate_hbm, w_gate), (w_up_hbm, w_up), (w_down_hbm, w_down))
        )
    ]
    for copy in weights:
        copy.start()
    greet_all(place, count)
    rows, width = hidden.shape
    cut = low.shape[-1]
    gather_scratch, first_scratch, second_scratch = rest[:6], rest[6:20], rest[20:]
    swaps = (place, attended, landed, swap_out, swap_in)
    sent = []
    for level in (4, 3, 2, 1, 0):
        sent.extend(swap_send(*swaps, level))
    landed[place.t] = attended[place.t]
    top = routes.shape[0]
    pick = (
        lax.broadcasted_iota(jnp.int32, (top, top), 0)
        == lax.broadcasted_iota(jnp.int32, (top, top), 1)
    ).astype(half)
    route_cols[...] = lax.dot_general(
        routes[...].astype(f32).astype(half), pick, (((0,), (0,)), ((), ())), preferred_element_type=f32
    ).reshape(count, rows, top)
    weights[0].wait()
    core_sent = []
    for level in (4, 3, 2, 1, 0):
        swap_wait(*swaps, level)
        blocks = place.blocks(level)
        heads = stage(stage_heads, landed, blocks)
        product = dot_rows(heads, w_out[...]).astype(half).reshape(len(blocks), rows, width)
        for i, block in enumerate(blocks):
            terms[block] = product[i]
        core_sent.extend(core_terms(place, terms, first_scratch, level))
    low_sum, high_sum = scatter_sums(place, terms, first_scratch, core_sent)
    for copy in sent:
        copy.wait_send()
    values = hidden[...].astype(f32)
    low_mid = (values[:, :cut] + low_sum).astype(half)
    high_mid = (values[:, cut:] + high_sum).astype(half)
    first, second = normalise(low_mid.astype(f32), high_mid.astype(f32), gain[...], width)
    low[place.t] = first
    high[place.t] = second
    for copy in weights[1:]:
        copy.wait()
    units = w_down.shape[0]
    expert = (place.t * units // EXPERT_HID).astype(f32)
    core_sent = []

    def experts(level):
        blocks = place.blocks(level)
        low_rows = stage(stage_low, low, blocks)
        high_rows = stage(stage_high, high, blocks)
        named = stage(stage_routes, route_cols, blocks)
        every = len(blocks) * rows

        def along(matrix):
            return dot_rows(low_rows, matrix[:, :cut]) + dot_rows(high_rows, matrix[:, cut:])

        logits = along(w_router)
        index = lax.broadcasted_iota(jnp.int32, (every, w_router.shape[0]), 1).astype(f32)
        names = [named[:, i : i + 1] for i in range(top)]
        picked = [
            jnp.sum(jnp.where(name == index, logits, 0.0), axis=1, keepdims=True) for name in names
        ]
        peak = functools.reduce(jnp.maximum, picked)
        shares = [jnp.exp(value - peak) for value in picked]
        total = functools.reduce(jnp.add, shares)
        gate_of = jnp.zeros_like(total)
        hit = jnp.zeros_like(total)
        for name, share in zip(names, shares):
            weight = (share / total).astype(half).astype(f32)
            gate_of = gate_of + jnp.where(name == expert, weight, 0.0)
            hit = hit + jnp.where(name == expert, 1.0, 0.0)
        gate = along(w_gate)
        up = along(w_up)
        active = (gate * jax.nn.sigmoid(SWIGLU_ALPHA * gate) * (up + 1.0)).astype(half)
        result = jnp.dot(active, w_down[...], preferred_element_type=f32)
        result = jnp.where(hit > 0.5, result * gate_of, 0.0).astype(half)
        result = result.reshape(len(blocks), rows, width)
        for i, block in enumerate(blocks):
            terms[block] = result[i]
        core_sent.extend(core_terms(place, terms, second_scratch, level))

    gather_rows(place, low, high, gather_scratch, experts)
    low_sum, high_sum = scatter_sums(place, terms, second_scratch, core_sent)
    out[:, :cut] = low_mid.astype(f32) + low_sum
    out[:, cut:] = high_mid.astype(f32) + high_sum


def layer(attended, hidden, gain, routes, w_router, w_out, w_gate, w_up, w_down):
    rows, width = hidden.shape
    count = attended.shape[0]
    cut = split_of(width)
    top = routes.shape[0]
    dma = pltpu.SemaphoreType.DMA
    half = jnp.bfloat16
    return pl.pallas_call(
        functools.partial(layer_kernel, count),
        out_shape=jax.ShapeDtypeStruct((rows, width), jnp.float32),
        in_specs=[vmem()] * 5 + [in_place()] * 4,
        out_specs=vmem(),
        scratch_shapes=[
            pltpu.VMEM(w_out.shape, half),
            pltpu.VMEM(w_gate.shape, half),
            pltpu.VMEM(w_up.shape, half),
            pltpu.VMEM(w_down.shape, half),
            dma((4,)),
            pltpu.VMEM(attended.shape, half),
            pltpu.VMEM((8, rows, attended.shape[2]), half),
            pltpu.VMEM((count, rows, width), half),
            pltpu.VMEM((count, rows, cut), half),
            pltpu.VMEM((count, rows, width - cut), half),
            pltpu.VMEM((8, rows, cut), half),
            pltpu.VMEM((8, rows, width - cut), half),
            pltpu.VMEM((count, rows, top), jnp.float32),
            pltpu.VMEM((8, rows, top), jnp.float32),
            dma((count,)),
            dma((count,)),
        ]
        + gather_sems()
        + scatter_scratch(rows, width)
        + scatter_scratch(rows, width),
        compiler_params=params(1),
        name="layer",
    )(attended, hidden, gain.reshape(1, width), routes, w_router, w_out, w_gate, w_up, w_down)


def local(
    hidden,
    attn_gain,
    w_query,
    w_keyval,
    w_out,
    cache_keys,
    cache_values,
    cache_lens,
    parents,
    accepted,
    moe_gain,
    w_router,
    routes,
    w_gate,
    w_up,
    w_down,
):
    devices = lax.axis_size("tp")
    projected = project(hidden, attn_gain, w_query, w_keyval.T, devices)
    attended, accepted_kv = attend(
        cache_lens, accepted, parents, projected, cache_keys, cache_values
    )
    layer_out = layer(
        attended, hidden, moe_gain, routes.T, w_router.T, w_out.T, w_gate, w_up, w_down
    )
    return (layer_out.astype(jnp.bfloat16), accepted_kv)


def solution(mesh):
    return jax.shard_map(
        local,
        mesh=mesh,
        in_specs=(
            P(("dp", "tp"), None),
            P(),
            P(None, "tp"),
            P(None, "tp"),
            P("tp", None),
            P(("dp", "tp"), None, None),
            P(("dp", "tp"), None, None),
            P(("dp", "tp")),
            P(("dp", "tp"), None),
            P(("dp", "tp")),
            P(),
            P(),
            P("dp", None),
            P("tp", None),
            P("tp", None),
            P("tp", None),
        ),
        out_specs=(P(("dp", "tp"), None), P(("dp", "tp"), None, None)),
        check_vma=False,
    )
```
